256 devices in a mesh: cells: 64 (over x, z, core), rhs: 4 (over y).
Axes of the slice: x: 4, y: 4, z: 8, core: 2. Of those that a mesh axis runs over, the one named last changes fastest.
Arguments:
- right_side: bfloat16 [512, 512, 384], P('cells', 'rhs'), may hold values from -6 to 6
- leaf_inverse: bfloat16 [512, 384, 384], P('cells'), may hold values from -0.3125 to 0.3125
- leaf_couple: bfloat16 [512, 9, 384, 128], P('cells'), may hold values from -0.3125 to 0.3125
- skel_target: int32 [512, 9], P('cells'), may hold values from 0 to 2047, as said below
- skeleton_in: float32 [512, 2048, 128], P('rhs', 'cells'), may hold values from -6 to 6
- lift_ops: bfloat16 [64, 4096, 512], P('cells', None, 'rhs'), may hold values from -0.09375 to 0.09375
- node_mix: bfloat16 [64, 1024, 512], P('cells', None, 'rhs'), may hold values from -0.1875 to 0.1875
- node_couple: bfloat16 [64, 512, 512], P('cells', None, 'rhs'), may hold values from -0.125 to 0.125
Outputs:
- leaf_solution: bfloat16 [512, 512, 384], P('cells', 'rhs')
- skeleton_rhs: float32 [512, 2048, 128], P('rhs', 'cells')
- node_solution: bfloat16 [64, 512, 512], P('cells', 'rhs')
- node_skeleton: float32 [64, 512, 512], P('cells', 'rhs')
The draws below stay inside these ranges and needn't reach their ends.
Inputs may be any that keep to these rules, and one draw needn't show every extreme that they name: `skel_target`: entry (c, k) names a skeleton block; its owner device, the entry // 32, lies at most 2 positions along cells from the cell's device c // 8, and on every device some slot reaches that distance.
All inputs are finite; a program needn't handle non-finite values.
Results may differ from the reference program's by a relative error of at most 0.03.
Values may be sent and summed in bfloat16 or wider, within the bound.
No kernel may reach another device: no remote copies, remote signals or barrier semaphores. Data moves between devices by JAX's collectives and lax.ppermute only.
A program may use at most 128 MiB of HBM per device.

```python
import jax
import jax.numpy as jnp
from jax import lax

SLOTS = 9
HOP = 2
CELLS_DEV = 8
RW = 384
SW = 128
MW = 512
SB = 32
SBW = 4096
NC = 512
NSB = 2048
COLS = 512
LEVELS = 6
N_CELLS = 64


def draw_skel_target(key, part):
    key_offset = jax.random.fold_in(key, 11)
    key_block = jax.random.fold_in(key, 23)
    cell_device = (jnp.arange(NC) // CELLS_DEV).astype(jnp.int32)
    offsets = jax.random.randint(key_offset, (NC, SLOTS), -HOP, HOP + 1).astype(jnp.int32)
    first_slot = (jnp.arange(NC) % CELLS_DEV == 0)[:, None] & (jnp.arange(SLOTS) == 0)[None, :]
    farthest = jnp.where(cell_device + HOP < N_CELLS, HOP, -HOP).astype(jnp.int32)
    offsets = jnp.where(first_slot, farthest[:, None], offsets)
    owner_dev = cell_device[:, None] + offsets
    owner_dev = jnp.where(owner_dev < 0, -owner_dev, owner_dev)
    owner_dev = jnp.where(owner_dev > N_CELLS - 1, 2 * (N_CELLS - 1) - owner_dev, owner_dev)
    block_pick = jax.random.randint(key_block, (NC, SLOTS), 0, SB).astype(jnp.int32)
    return (owner_dev * SB + block_pick).astype(jnp.int32)


def level_of(rng, dims, pieces, smallest, high):
    loudness = 1.0
    for axis_at, parts in pieces:
        draws = jax.random.uniform(jax.random.fold_in(jax.random.fold_in(rng, 6), axis_at), (parts,), jnp.float32, smallest / len(pieces), high / len(pieces))
        loudness = loudness * jnp.repeat(jnp.exp(draws), dims[axis_at] // parts).reshape((-1,) + (1,) * (len(dims) - 1 - axis_at))
    return loudness


def gaussian(rng, dims, width, limit, cuts=(), dtype=jnp.bfloat16):
    drawn = width * jax.random.normal(rng, dims, jnp.float32)
    if cuts:
        drawn = drawn * level_of(rng, dims, cuts, -0.22, 0.18)
    return jnp.clip(drawn, -limit, limit).astype(dtype)


def setup_inputs(seed: int = 0) -> dict:
    streams_of = jax.random.split(jax.random.key(seed), 9)
    return {
        "right_side": gaussian(streams_of[0], (NC, COLS, RW), 1.0, 6.0, ((0, 64), (1, 4))),
        "leaf_inverse": gaussian(streams_of[1], (NC, RW, RW), RW ** -0.5, 0.3125, ((0, 64),)),
        "leaf_couple": gaussian(streams_of[2], (NC, SLOTS, RW, SW), RW ** -0.5, 0.3125, ((0, 64),)),
        "skel_target": draw_skel_target(jax.random.fold_in(streams_of[8], 71), 0),
        "skeleton_in": gaussian(streams_of[4], (COLS, NSB, SW), 1.0, 6.0, ((0, 4), (1, 64)), jnp.float32),
        "lift_ops": gaussian(streams_of[5], (N_CELLS, SBW, MW), SBW ** -0.5, 0.09375, ((0, 64), (2, 4))),
        "node_mix": gaussian(streams_of[6], (N_CELLS, 2 * MW, MW), (2 * MW) ** -0.5, 0.1875, ((0, 64), (2, 4))),
        "node_couple": gaussian(streams_of[7], (N_CELLS, MW, MW), (4 * MW) ** -0.5, 0.125, ((0, 64), (2, 4))),
    }


def leaf_step(operands):
    rhs_cell, inverse_cell, couple_cell = operands
    solved = jnp.dot(rhs_cell, inverse_cell, preferred_element_type=jnp.float32).astype(jnp.bfloat16)
    updates = jnp.einsum("cr,krs->kcs", solved.astype(jnp.float32), couple_cell.astype(jnp.float32))
    return solved, updates


def lift_step(operands):
    flattened, lift_cell = operands
    return jnp.dot(flattened, lift_cell, preferred_element_type=jnp.float32).astype(jnp.bfloat16)


def combine(left_child, right_child, mix_ops, couple_ops):
    joined = jnp.concatenate([left_child, right_child], axis=-1)
    solution = jnp.einsum("ncw,nwm->ncm", joined.astype(jnp.float32), mix_ops.astype(jnp.float32)).astype(jnp.bfloat16)
    coupled = jnp.einsum("ncw,nwm->ncm", solution.astype(jnp.float32), couple_ops.astype(jnp.float32))
    skeleton = 0.5 * (left_child.astype(jnp.float32) + right_child.astype(jnp.float32)) - coupled
    return solution, skeleton


def reference(right_side, leaf_inverse, leaf_couple, skel_target, skeleton_in, lift_ops, node_mix, node_couple):
    solved, updates = lax.map(leaf_step, (right_side, leaf_inverse, leaf_couple))
    summed = jax.ops.segment_sum(updates.reshape(NC * SLOTS, COLS, SW), skel_target.reshape(NC * SLOTS), num_segments=NSB)
    skeleton_rhs = skeleton_in - jnp.transpose(summed, (1, 0, 2))
    flattened = jnp.transpose(skeleton_rhs.reshape(COLS, N_CELLS, SBW), (1, 0, 2)).astype(jnp.bfloat16)
    carried = lax.map(lift_step, (flattened, lift_ops))
    level_solution = jnp.zeros((N_CELLS, COLS, MW), jnp.bfloat16)
    for section_level in range(1, LEVELS + 1):
        if section_level == 1:
            left_child = jnp.roll(carried, 1, axis=0)
            right_child = carried
        else:
            distance = 2 ** (section_level - 2)
            left_child = jnp.roll(carried, distance, axis=0)
            right_child = jnp.roll(carried, -distance, axis=0)
        level_solution, skeleton = combine(left_child, right_child, node_mix, node_couple)
        carried = skeleton.astype(jnp.bfloat16)
    middle = N_CELLS // 2
    node_solution, node_skeleton = combine(jnp.roll(carried, -middle, axis=0), jnp.roll(level_solution, -middle, axis=0), node_mix, node_couple)
    return solved, skeleton_rhs, node_solution, node_skeleton
```

```python
import functools

import jax
import jax.numpy as jnp
from jax import lax
from jax.experimental import pallas as pl
from jax.experimental.pallas import tpu as pltpu
from jax.sharding import PartitionSpec as P

HOP = 2
BF16 = jnp.bfloat16
F32 = jnp.float32


def dot32(a, b):
    return jnp.dot(a, b, preferred_element_type=F32)


def shifted(value, axis, by):
    count = lax.axis_size(axis)
    return lax.ppermute(value, axis, [(i, (i + by) % count) for i in range(count)])


def along_pairs(value, pairs):
    count = lax.axis_size("cells")
    return lax.ppermute(value, "cells", [(a, b) for a, b in pairs if 0 <= b < count])


def leaf_kernel(slots, blocks, index_ref, roles_ref, rs_ref, inv_ref, couple_ref,
                sol_ref, own_ref, far_ref, near_ref, swap_ref, acc):
    cell = pl.program_id(0)

    @pl.when(cell == 0)
    def _():
        @pl.loop(0, acc.shape[0])
        def _(b):
            acc[b] = jnp.zeros(acc.shape[1:], F32)

    solved = dot32(rs_ref[0], inv_ref[0]).astype(BF16)
    sol_ref[0] = solved
    width = couple_ref.shape[3]
    for first in range(0, slots, 2):
        group = range(first, min(first + 2, slots))
        operators = [couple_ref[0, k] for k in group]
        joined = operators[0] if len(operators) == 1 else jnp.concatenate(operators, axis=1)
        update = dot32(solved, joined)
        for n, k in enumerate(group):
            target = index_ref[cell * slots + k]
            acc[target] += update[:, n * width : (n + 1) * width]

    @pl.when(cell == pl.num_programs(0) - 1)
    def _():
        @pl.loop(0, blocks)
        def _(b):
            own_ref[b] = acc[HOP * blocks + b]
            far_ref[b] = acc[roles_ref[0] * blocks + b].astype(BF16)
            near_ref[b] = acc[roles_ref[1] * blocks + b].astype(BF16)
            swap_ref[0, b] = acc[roles_ref[2] * blocks + b].astype(BF16)
            swap_ref[1, b] = acc[roles_ref[3] * blocks + b].astype(BF16)


def leaf_phase(index, roles, right_side, leaf_inverse, leaf_couple, blocks):
    cells, rows, width = right_side.shape
    slots, sw = leaf_couple.shape[1], leaf_couple.shape[3]
    spans = 2 * HOP + 1
    whole3 = lambda i, *_: (0, 0, 0)
    whole4 = lambda i, *_: (0, 0, 0, 0)
    return pl.pallas_call(
        functools.partial(leaf_kernel, slots, blocks),
        out_shape=(
            jax.ShapeDtypeStruct((cells, rows, width), BF16),
            jax.ShapeDtypeStruct((blocks, rows, sw), F32),
            jax.ShapeDtypeStruct((blocks, rows, sw), BF16),
            jax.ShapeDtypeStruct((blocks, rows, sw), BF16),
            jax.ShapeDtypeStruct((2, blocks, rows, sw), BF16),
        ),
        grid_spec=pltpu.PrefetchScalarGridSpec(
            num_scalar_prefetch=2,
            grid=(cells,),
            in_specs=[
                pl.BlockSpec((1, rows, width), lambda i, *_: (i, 0, 0)),
                pl.BlockSpec((1, width, width), lambda i, *_: (i, 0, 0)),
                pl.BlockSpec((1, slots, width, sw), lambda i, *_: (i, 0, 0, 0)),
            ],
            out_specs=[
                pl.BlockSpec((1, rows, width), lambda i, *_: (i, 0, 0)),
                pl.BlockSpec((blocks, rows, sw), whole3, pipeline_mode=pl.Buffered(1)),
                pl.BlockSpec((blocks, rows, sw), whole3, pipeline_mode=pl.Buffered(1)),
                pl.BlockSpec((blocks, rows, sw), whole3, pipeline_mode=pl.Buffered(1)),
                pl.BlockSpec((2, blocks, rows, sw), whole4, pipeline_mode=pl.Buffered(1)),
            ],
            scratch_shapes=[pltpu.VMEM((spans * blocks, rows, sw), F32)],
        ),
        compiler_params=pltpu.CompilerParams(vmem_limit_bytes=40 << 20),
        cost_estimate=pl.CostEstimate(flops=1_300_000_000, bytes_accessed=17_000_000, transcendentals=0),
        name="leaf",
    )(index, roles, right_side, leaf_inverse, leaf_couple)


def lift_kernel(base_ref, far_ref, near_ref, own_ref, prev_ref, next_ref, opp_lo_ref, opp_hi_ref,
                place_ref, out_ref, acc):
    step = pl.program_id(0)

    @pl.when(step == 0)
    def _():
        acc[...] = jnp.zeros_like(acc)

    count, width = base_ref.shape[1], base_ref.shape[3]
    total = acc[...]
    for half, opp_ref in ((0, opp_lo_ref), (1, opp_hi_ref)):
        parts = []
        for b in range(count):
            value = base_ref[half, b] - far_ref[half, b].astype(F32) - near_ref[half, b].astype(F32)
            parts.append(value.astype(BF16))
        left = jnp.concatenate(parts, axis=1)
        right = jnp.concatenate([own_ref[half], prev_ref[half], next_ref[half], opp_ref[...]], axis=1)
        total = total + dot32(left, right)
    acc[...] = total

    @pl.when(step == pl.num_programs(0) - 1)
    def _():
        sw = own_ref.shape[2]
        for j in range(4):
            at = pl.multiple_of(place_ref[j] * sw, sw)
            out_ref[:, pl.ds(at, sw)] = acc[:, j * sw : (j + 1) * sw].astype(BF16)


def lift_phase(base, far, near, pieces, place):
    own, prev, nxt, opp_lo, opp_hi = pieces
    blocks, rows, width = base.shape
    steps = 4
    per = blocks // 2 // steps
    depth = per * width
    cols = own.shape[1]
    split = lambda v: v.reshape(2, blocks // 2, rows, width)
    halves = lambda v: v.reshape(2, v.shape[0] // 2, cols)
    block_spec = pl.BlockSpec((2, per, rows, width), lambda i: (0, i, 0, 0))
    op_spec = pl.BlockSpec((2, depth, cols), lambda i: (0, i, 0))
    opp_spec = pl.BlockSpec((depth, cols), lambda i: (i, 0))
    return pl.pallas_call(
        lift_kernel,
        out_shape=jax.ShapeDtypeStruct((rows, 4 * cols), BF16),
        grid=(steps,),
        in_specs=[block_spec] * 3 + [op_spec] * 3 + [opp_spec] * 2 + [pl.BlockSpec(memory_space=pltpu.SMEM)],
        out_specs=pl.BlockSpec((rows, 4 * cols), lambda i: (0, 0)),
        scratch_shapes=[pltpu.VMEM((rows, 4 * cols), F32)],
        compiler_params=pltpu.CompilerParams(vmem_limit_bytes=24 << 20),
        cost_estimate=pl.CostEstimate(flops=540_000_000, bytes_accessed=8_000_000, transcendentals=0),
        name="lift",
    )(split(base), split(far), split(near), halves(own), halves(prev), halves(nxt), opp_lo, opp_hi, place)


def assemble_kernel(with_product, own_ref, prev_ref, next_ref, opp_lo_ref, opp_hi_ref, place_ref, ops_ref, *rest):
    sw = own_ref.shape[1]
    half = opp_lo_ref.shape[0]
    for j, ref in enumerate((own_ref, prev_ref, next_ref)):
        ops_ref[:, pl.ds(pl.multiple_of(place_ref[j] * sw, sw), sw)] = ref[...]
    at = pl.multiple_of(place_ref[3] * sw, sw)
    ops_ref[pl.ds(0, half), pl.ds(at, sw)] = opp_lo_ref[...]
    ops_ref[pl.ds(half, half), pl.ds(at, sw)] = opp_hi_ref[...]
    if with_product:
        (product_ref,) = rest
        width = ops_ref.shape[1]
        for r in range(0, 2 * width, width // 2):
            rows = pl.ds(r, width // 2)
            product_ref[rows, :] = (-dot32(ops_ref[rows, :], ops_ref[pl.ds(2 * width, width), :])).astype(BF16)


def assemble(pieces, place, with_product):
    depth, cols = pieces[0].shape
    outs = [jax.ShapeDtypeStruct((depth, 4 * cols), BF16)]
    if with_product:
        outs.append(jax.ShapeDtypeStruct((8 * cols, 4 * cols), BF16))
    vmem = pl.BlockSpec(memory_space=pltpu.VMEM)
    return pl.pallas_call(
        functools.partial(assemble_kernel, with_product),
        out_shape=tuple(outs),
        in_specs=[vmem] * 5 + [pl.BlockSpec(memory_space=pltpu.SMEM)],
        out_specs=tuple([vmem] * len(outs)),
        compiler_params=pltpu.CompilerParams(vmem_limit_bytes=16 << 20),
        cost_estimate=pl.CostEstimate(
            flops=540_000_000 if with_product else 0, bytes_accessed=4_000_000, transcendentals=0
        ),
        name="assemble_product" if with_product else "assemble",
    )(*pieces, place)


def top_kernel(first_ref, second_ref, ops_q_ref, ops_p_ref, sol_ref, skel_ref):
    width = first_ref.shape[1]

    def merge(first, second, ops_ref):
        sol = (dot32(first, ops_ref[pl.ds(0, width), :]) + dot32(second, ops_ref[pl.ds(width, width), :])).astype(BF16)
        skel = 0.5 * (first.astype(F32) + second.astype(F32)) - dot32(sol, ops_ref[pl.ds(2 * width, width), :])
        return sol, skel

    level_sol, level_skel = merge(first_ref[...], second_ref[...], ops_q_ref)
    sol, skel = merge(level_skel.astype(BF16), level_sol, ops_p_ref)
    sol_ref[...] = sol
    skel_ref[...] = skel


def top_phase(first, second, ops_q, ops_p):
    rows, width = first.shape
    vmem = pl.BlockSpec(memory_space=pltpu.VMEM)
    return pl.pallas_call(
        top_kernel,
        out_shape=(jax.ShapeDtypeStruct((rows, width), BF16), jax.ShapeDtypeStruct((rows, width), F32)),
        in_specs=[vmem] * 4,
        out_specs=(vmem, vmem),
        compiler_params=pltpu.CompilerParams(vmem_limit_bytes=16 << 20),
        cost_estimate=pl.CostEstimate(flops=400_000_000, bytes_accessed=4_000_000, transcendentals=0),
        name="top",
    )(first, second, ops_q, ops_p)


def around_rhs(value):
    half = value.shape[0] // 2
    prev = shifted(value, "rhs", 1)
    nxt = shifted(value, "rhs", -1)
    opp_lo = shifted(prev[:half], "rhs", 1)
    opp_hi = shifted(nxt[half:], "rhs", -1)
    return value, prev, nxt, opp_lo, opp_hi


def on_device(
    right_side, leaf_inverse, leaf_couple, skel_target, skeleton_in, lift_ops, node_mix, node_couple
):
    count = lax.axis_size("cells")
    position = lax.axis_index("cells")
    column = lax.axis_index("rhs")
    levels = count.bit_length() - 1
    rows, blocks, width = skeleton_in.shape
    core = position % 2

    place = jnp.stack([column, (column + 3) % 4, (column + 1) % 4, (column + 2) % 4]).astype(jnp.int32)
    lift_pieces = around_rhs(lift_ops[0])
    node_ops = jnp.concatenate([node_mix[0], node_couple[0]], axis=0)
    across = shifted(node_ops, "cells", count // 2)

    targets = skel_target.reshape(-1)
    index = (targets - (position - HOP) * blocks).astype(jnp.int32)
    roles = jnp.where(core == 1, jnp.array([4, 3, 1, 0], jnp.int32), jnp.array([0, 1, 3, 4], jnp.int32))
    solved, own, far, near, swap = leaf_phase(index, roles, right_side, leaf_inverse, leaf_couple, blocks)

    half = range(count // 2)
    far_in = along_pairs(far, [(2 * c + 1, 2 * c + 3) for c in half] + [(2 * c, 2 * c - 2) for c in half])
    swapped = along_pairs(swap, [(2 * c, 2 * c + 1) for c in half] + [(2 * c + 1, 2 * c) for c in half])
    near = (near.astype(F32) + swapped[1].astype(F32)).astype(BF16)
    near_in = along_pairs(near, [(2 * c + 1, 2 * c + 2) for c in half] + [(2 * c, 2 * c - 1) for c in half])

    base = jnp.transpose(skeleton_in, (1, 0, 2)) - own - swapped[0].astype(F32)
    current = lift_phase(base, far_in, near_in, lift_pieces, place)
    final = base - far_in.astype(F32) - near_in.astype(F32)
    skeleton_rhs = jnp.transpose(final, (1, 0, 2))

    ops_p, product = assemble(around_rhs(node_ops), place, True)
    (ops_q,) = assemble(around_rhs(across), place, False)
    mw = current.shape[1]
    for level in range(1, levels):
        distance = max(1, 2 ** (level - 2))
        first = shifted(current, "cells", distance)
        second = current if level == 1 else shifted(current, "cells", -distance)
        skel = 0.5 * (first.astype(F32) + second.astype(F32)) + (
            dot32(first, product[:mw]) + dot32(second, product[mw:])
        )
        current = skel.astype(BF16)
    distance = 2 ** (levels - 2)
    second = shifted(current, "cells", distance)
    first = shifted(current, "cells", -distance)
    node_solution, node_skeleton = top_phase(first, second, ops_q, ops_p)
    return (solved, skeleton_rhs, node_solution[None], node_skeleton[None])


def solution(mesh):
    return jax.shard_map(
        on_device,
        mesh=mesh,
        in_specs=(
            P("cells", "rhs", None),
            P("cells", None, None),
            P("cells", None, None, None),
            P("cells", None),
            P("rhs", "cells", None),
            P("cells", None, "rhs"),
            P("cells", None, "rhs"),
            P("cells", None, "rhs"),
        ),
        out_specs=(
            P("cells", "rhs", None),
            P("rhs", "cells", None),
            P("cells", "rhs", None),
            P("cells", "rhs", None),
        ),
        check_vma=False,
    )
```

```python
import functools

import jax
import jax.numpy as jnp
from jax import lax
from jax.experimental import pallas as pl
from jax.experimental.pallas import tpu as pltpu
from jax.sharding import PartitionSpec as P

HOP = 2
DEST_PARTS = (24, 8)
RED_PARTS = (16, 16)
BF16 = jnp.bfloat16
F32 = jnp.float32


def dot32(a, b):
    return jnp.dot(a, b, preferred_element_type=F32)


def shifted(value, axis, by):
    count = lax.axis_size(axis)
    return lax.ppermute(value, axis, [(i, (i + by) % count) for i in range(count)])


def along_pairs(value, pairs):
    count = lax.axis_size("cells")
    return lax.ppermute(value, "cells", [(a, b) for a, b in pairs if 0 <= b < count])


def copy_parts(acc, start, refs):
    first = 0
    for ref in refs:

        @pl.loop(0, ref.shape[0])
        def _(b, ref=ref, first=first):
            ref[b] = acc[start + first + b].astype(BF16)

        first += ref.shape[0]


def leaf_kernel(cells, slots, blocks, target_ref, rs_ref, inv_ref, couple_ref,
                sol_ref, own_ref, far_ref, near_ref, *refs):
    *part_refs, acc = refs
    step = pl.program_id(0)
    position = lax.axis_index("cells")
    shift = (position - HOP) * blocks

    @pl.when(step == 0)
    def _():
        @pl.loop(0, acc.shape[0])
        def _(b):
            acc[b] = jnp.zeros(acc.shape[1:], F32)

    width = couple_ref.shape[3]
    solved = []
    for c in range(cells):
        value = dot32(rs_ref[c], inv_ref[c]).astype(BF16)
        sol_ref[c] = value
        solved.append(value)
    for c in range(cells):
        for first in range(0, slots, 2):
            group = range(first, min(first + 2, slots))
            operators = [couple_ref[c, k] for k in group]
            joined = operators[0] if len(operators) == 1 else jnp.concatenate(operators, axis=1)
            update = dot32(solved[c], joined)
            for n, k in enumerate(group):
                target = target_ref[step * cells + c, k] - shift
                acc[target] += update[:, n * width : (n + 1) * width]

    @pl.when(step == pl.num_programs(0) - 1)
    def _():
        odd = position % 2
        spans = 2 * HOP
        far, near, dest, red = (
            jnp.where(odd == 1, spans - k, k) * blocks for k in (0, 1, HOP + 1, 2 * HOP)
        )

        @pl.loop(0, blocks)
        def _(b):
            own_ref[b] = acc[HOP * blocks + b]
            far_ref[b] = acc[far + b].astype(BF16)
            near_ref[b] = acc[near + b].astype(BF16)

        copy_parts(acc, dest, part_refs[: len(DEST_PARTS)])
        copy_parts(acc, red, part_refs[len(DEST_PARTS) :])


def leaf_phase(targets, right_side, leaf_inverse, leaf_couple, blocks, per_step=4):
    cells, rows, width = right_side.shape
    slots, sw = leaf_couple.shape[1], leaf_couple.shape[3]
    spans = 2 * HOP + 1
    whole = lambda i, *_: (0, 0, 0)
    by_cell = lambda i, *_: (i, 0, 0)
    summed = pl.BlockSpec((blocks, rows, sw), whole, pipeline_mode=pl.Buffered(1))
    parts = [blocks * n // 32 for n in DEST_PARTS + RED_PARTS]
    return pl.pallas_call(
        functools.partial(leaf_kernel, per_step, slots, blocks),
        out_shape=(
            jax.ShapeDtypeStruct((cells, rows, width), BF16),
            jax.ShapeDtypeStruct((blocks, rows, sw), F32),
        )
        + (jax.ShapeDtypeStruct((blocks, rows, sw), BF16),) * 2
        + tuple(jax.ShapeDtypeStruct((n, rows, sw), BF16) for n in parts),
        grid_spec=pltpu.PrefetchScalarGridSpec(
            num_scalar_prefetch=1,
            grid=(cells // per_step,),
            in_specs=[
                pl.BlockSpec((per_step, rows, width), by_cell),
                pl.BlockSpec((per_step, width, width), by_cell),
                pl.BlockSpec((per_step, slots, width, sw), lambda i, *_: (i, 0, 0, 0)),
            ],
            out_specs=[pl.BlockSpec((per_step, rows, width), by_cell)] + [summed] * 3
            + [pl.BlockSpec((n, rows, sw), whole, pipeline_mode=pl.Buffered(1)) for n in parts],
            scratch_shapes=[pltpu.VMEM((spans * blocks, rows, sw), F32)],
        ),
        compiler_params=pltpu.CompilerParams(vmem_limit_bytes=60 << 20),
        cost_estimate=pl.CostEstimate(flops=0, bytes_accessed=0, transcendentals=0),
        name="leaf",
    )(targets, right_side, leaf_inverse, leaf_couple)


def add_kernel(near_ref, *refs):
    *part_refs, out_ref = refs
    at = 0
    for ref in part_refs:
        count = ref.shape[0]
        mine = near_ref[pl.ds(at, count)].astype(F32)
        out_ref[pl.ds(at, count)] = (mine + ref[...].astype(F32)).astype(BF16)
        at += count


def add_parts(near, *parts):
    vmem = pl.BlockSpec(memory_space=pltpu.VMEM)
    return pl.pallas_call(
        add_kernel,
        out_shape=jax.ShapeDtypeStruct(near.shape, BF16),
        in_specs=[vmem] * (1 + len(parts)),
        out_specs=vmem,
        compiler_params=pltpu.CompilerParams(vmem_limit_bytes=16 << 20),
        cost_estimate=pl.CostEstimate(flops=0, bytes_accessed=0, transcendentals=0),
        name="add_parts",
    )(near, *parts)


def lift_kernel(base_ref, far_ref, near_ref, own_ref, prev_ref, next_ref, opp_lo_ref, opp_hi_ref, out_ref):
    blocks, rows, width = base_ref.shape
    sw = own_ref.shape[1]
    deep = opp_lo_ref.shape[0]
    depth = 2 * width
    column = lax.axis_index("rhs")
    total = jnp.zeros((rows, 4 * sw), F32)
    for b in range(0, blocks, 2):
        parts = [
            (base_ref[k] - far_ref[k].astype(F32) - near_ref[k].astype(F32)).astype(BF16) for k in (b, b + 1)
        ]
        row = b * width
        pieces = [ref[row : row + depth, :] for ref in (own_ref, prev_ref, next_ref)]
        opp_ref = (opp_lo_ref, opp_hi_ref)[row // deep]
        pieces.append(opp_ref[row % deep : row % deep + depth, :])
        total = total + dot32(jnp.concatenate(parts, axis=1), jnp.concatenate(pieces, axis=1))
    result = total.astype(BF16)
    for j, turn in enumerate((0, 3, 1, 2)):
        at = pl.multiple_of((column + turn) % 4 * sw, sw)
        out_ref[:, pl.ds(at, sw)] = result[:, j * sw : (j + 1) * sw]


def lift_phase(*operands):
    rows, cols = operands[0].shape[1], operands[3].shape[1]
    vmem = pl.BlockSpec(memory_space=pltpu.VMEM)
    return pl.pallas_call(
        lift_kernel,
        out_shape=jax.ShapeDtypeStruct((rows, 4 * cols), BF16),
        in_specs=[vmem] * len(operands),
        out_specs=vmem,
        compiler_params=pltpu.CompilerParams(vmem_limit_bytes=24 << 20),
        cost_estimate=pl.CostEstimate(flops=0, bytes_accessed=0, transcendentals=0),
        name="lift",
    )(*operands)


def assemble_kernel(with_product, own_ref, prev_ref, next_ref, opp_ref, ops_ref, *rest):
    sw = own_ref.shape[1]
    column = lax.axis_index("rhs")
    for turn, ref in ((0, own_ref), (3, prev_ref), (1, next_ref), (2, opp_ref)):
        ops_ref[:, pl.ds(pl.multiple_of((column + turn) % 4 * sw, sw), sw)] = ref[...]
    if with_product:
        (product_ref,) = rest
        width = ops_ref.shape[1]
        for r in range(0, 2 * width, width // 2):
            rows = pl.ds(r, width // 2)
            product_ref[rows, :] = (-dot32(ops_ref[rows, :], ops_ref[pl.ds(2 * width, width), :])).astype(BF16)


def assemble(pieces, with_product):
    depth, cols = pieces[0].shape
    outs = [jax.ShapeDtypeStruct((depth, 4 * cols), BF16)]
    if with_product:
        outs.append(jax.ShapeDtypeStruct((8 * cols, 4 * cols), BF16))
    vmem = pl.BlockSpec(memory_space=pltpu.VMEM)
    return pl.pallas_call(
        functools.partial(assemble_kernel, with_product),
        out_shape=tuple(outs),
        in_specs=[vmem] * 4,
        out_specs=tuple([vmem] * len(outs)),
        compiler_params=pltpu.CompilerParams(vmem_limit_bytes=16 << 20),
        cost_estimate=pl.CostEstimate(
            flops=0, bytes_accessed=0, transcendentals=0
        ),
        name="assemble_product" if with_product else "assemble",
    )(*pieces)


def top_kernel(first_ref, second_ref, ops_q_ref, ops_p_ref, sol_ref, skel_ref):
    width = first_ref.shape[1]

    def merge(first, second, ops_ref):
        sol = (dot32(first, ops_ref[pl.ds(0, width), :]) + dot32(second, ops_ref[pl.ds(width, width), :])).astype(BF16)
        skel = 0.5 * (first.astype(F32) + second.astype(F32)) - dot32(sol, ops_ref[pl.ds(2 * width, width), :])
        return sol, skel

    level_sol, level_skel = merge(first_ref[...], second_ref[...], ops_q_ref)
    sol, skel = merge(level_skel.astype(BF16), level_sol, ops_p_ref)
    sol_ref[...] = sol
    skel_ref[...] = skel


def top_phase(first, second, ops_q, ops_p):
    rows, width = first.shape
    vmem = pl.BlockSpec(memory_space=pltpu.VMEM)
    return pl.pallas_call(
        top_kernel,
        out_shape=(jax.ShapeDtypeStruct((rows, width), BF16), jax.ShapeDtypeStruct((rows, width), F32)),
        in_specs=[vmem] * 4,
        out_specs=(vmem, vmem),
        compiler_params=pltpu.CompilerParams(vmem_limit_bytes=16 << 20),
        cost_estimate=pl.CostEstimate(flops=400_000_000, bytes_accessed=4_000_000, transcendentals=0),
        name="top",
    )(first, second, ops_q, ops_p)


def on_device(
    right_side, leaf_inverse, leaf_couple, skel_target, skeleton_in, lift_ops, node_mix, node_couple
):
    count = lax.axis_size("cells")
    levels = count.bit_length() - 1
    rows, blocks, width = skeleton_in.shape

    lift = lift_ops[0]
    deep = lift.shape[0] // 2
    prev = shifted(lift, "rhs", 1)
    following = shifted(lift, "rhs", -1)

    solved, own, far, near, *parts = leaf_phase(skel_target, right_side, leaf_inverse, leaf_couple, blocks)

    half = range(count // 2)
    swap = [(2 * c, 2 * c + 1) for c in half] + [(2 * c + 1, 2 * c) for c in half]
    dest, red = parts[: len(DEST_PARTS)], parts[len(DEST_PARTS) :]
    red_in = [along_pairs(part, swap) for part in red]
    far_in = along_pairs(far, [(2 * c + 1, 2 * c + 3) for c in half] + [(2 * c, 2 * c - 2) for c in half])
    near = add_parts(near, *red_in)
    near_in = along_pairs(near, [(2 * c + 1, 2 * c + 2) for c in half] + [(2 * c, 2 * c - 1) for c in half])

    *dest, prev, following = lax.optimization_barrier((*dest, prev, following))
    opp_lo = shifted(prev[:deep], "rhs", 1)
    opp_hi = shifted(following[deep:], "rhs", -1)
    dest_in = jnp.concatenate([along_pairs(part, swap) for part in dest], axis=0)
    dest_in, far_in, near_in = lax.optimization_barrier((dest_in, far_in, near_in))
    base = lax.optimization_barrier(jnp.transpose(skeleton_in, (1, 0, 2)) - own - dest_in.astype(F32))
    current = lift_phase(base, far_in, near_in, lift, prev, following, opp_lo, opp_hi)
    base_after, far_after, near_after, _ = lax.optimization_barrier((base, far_in, near_in, current))
    skeleton_rhs = jnp.transpose(base_after - far_after.astype(F32) - near_after.astype(F32), (1, 0, 2))

    mix, couple, _ = lax.optimization_barrier((node_mix, node_couple, near))
    node_ops = jnp.concatenate([mix[0], couple[0]], axis=0)
    node_ops, _ = lax.optimization_barrier((node_ops, base))
    ops_prev = shifted(node_ops, "rhs", 1)
    ops_next = shifted(node_ops, "rhs", -1)
    node_ops, _, _ = lax.optimization_barrier((node_ops, opp_lo, opp_hi))
    across = shifted(node_ops, "cells", count // 2)
    ops_opp = shifted(node_ops, "rhs", 2)
    ops_p, product = assemble((node_ops, ops_prev, ops_next, ops_opp), True)

    mw = current.shape[1]
    for level in range(1, levels):
        distance = max(1, 2 ** (level - 2))
        first = shifted(current, "cells", distance)
        second = current if level == 1 else shifted(current, "cells", -distance)
        if level == 1:
            first, product, across = lax.optimization_barrier((first, product, across))
        if level == levels - 1:
            first, ops_q = lax.optimization_barrier((first, ops_q))
        skel = 0.5 * (first.astype(F32) + second.astype(F32)) + (
            dot32(first, product[:mw]) + dot32(second, product[mw:])
        )
        current = skel.astype(BF16)
        if level == 2:
            across, _ = lax.optimization_barrier((across, current))
            ops_q = assemble((across, *(shifted(across, "rhs", turn) for turn in (1, -1, 2))), False)[0]
    distance = 2 ** (levels - 2)
    second = shifted(current, "cells", distance)
    first = shifted(current, "cells", -distance)
    node_solution, node_skeleton = top_phase(first, second, ops_q, ops_p)
    return (solved, skeleton_rhs, node_solution[None], node_skeleton[None])


def solution(mesh):
    return jax.shard_map(
        on_device,
        mesh=mesh,
        in_specs=(
            P("cells", "rhs", None),
            P("cells", None, None),
            P("cells", None, None, None),
            P("cells", None),
            P("rhs", "cells", None),
            P("cells", None, "rhs"),
            P("cells", None, "rhs"),
            P("cells", None, "rhs"),
        ),
        out_specs=(
            P("cells", "rhs", None),
            P("rhs", "cells", None),
            P("cells", "rhs", None),
            P("cells", "rhs", None),
        ),
        check_vma=False,
    )
```

```python
import functools

import jax
import jax.numpy as jnp
from jax import lax
from jax.experimental import pallas as pl
from jax.experimental.pallas import tpu as pltpu
from jax.sharding import PartitionSpec as P

HOP = 2
DEST_PARTS = (24, 8)
RED_PARTS = (16, 16)
BF16 = jnp.bfloat16
F32 = jnp.float32


def dot32(a, b):
    return jnp.dot(a, b, preferred_element_type=F32)


def shifted(value, axis, by):
    count = lax.axis_size(axis)
    return lax.ppermute(value, axis, [(i, (i + by) % count) for i in range(count)])


def along_pairs(value, pairs):
    count = lax.axis_size("cells")
    return lax.ppermute(value, "cells", [(a, b) for a, b in pairs if 0 <= b < count])


def copy_parts(acc, start, refs):
    first = 0
    for ref in refs:

        @pl.loop(0, ref.shape[0])
        def _(b, ref=ref, first=first):
            ref[b] = acc[start + first + b].astype(BF16)

        first += ref.shape[0]


def leaf_kernel(cells, slots, blocks, target_ref, rs_ref, inv_ref, couple_ref,
                sol_ref, own_ref, far_ref, near_ref, *refs):
    *part_refs, acc = refs
    step = pl.program_id(0)
    position = lax.axis_index("cells")
    shift = (position - HOP) * blocks

    @pl.when(step == 0)
    def _():
        @pl.loop(0, acc.shape[0])
        def _(b):
            acc[b] = jnp.zeros(acc.shape[1:], F32)

    width = couple_ref.shape[3]
    solved = []
    for c in range(cells):
        value = dot32(rs_ref[c], inv_ref[c]).astype(BF16)
        sol_ref[c] = value
        solved.append(value)
    for c in range(cells):
        for first in range(0, slots, 2):
            group = range(first, min(first + 2, slots))
            operators = [couple_ref[c, k] for k in group]
            joined = operators[0] if len(operators) == 1 else jnp.concatenate(operators, axis=1)
            update = dot32(solved[c], joined)
            for n, k in enumerate(group):
                target = target_ref[step * cells + c, k] - shift
                acc[target] += update[:, n * width : (n + 1) * width]

    @pl.when(step == pl.num_programs(0) - 1)
    def _():
        odd = position % 2
        spans = 2 * HOP
        far, near, dest, red = (
            jnp.where(odd == 1, spans - k, k) * blocks for k in (0, 1, HOP + 1, 2 * HOP)
        )

        @pl.loop(0, blocks)
        def _(b):
            own_ref[b] = acc[HOP * blocks + b]
            far_ref[b] = acc[far + b].astype(BF16)
            near_ref[b] = acc[near + b].astype(BF16)

        copy_parts(acc, dest, part_refs[: len(DEST_PARTS)])
        copy_parts(acc, red, part_refs[len(DEST_PARTS) :])


def leaf_phase(targets, right_side, leaf_inverse, leaf_couple, blocks, per_step=4):
    cells, rows, width = right_side.shape
    slots, sw = leaf_couple.shape[1], leaf_couple.shape[3]
    spans = 2 * HOP + 1
    whole = lambda i, *_: (0, 0, 0)
    by_cell = lambda i, *_: (i, 0, 0)
    summed = pl.BlockSpec((blocks, rows, sw), whole, pipeline_mode=pl.Buffered(1))
    parts = [blocks * n // 32 for n in DEST_PARTS + RED_PARTS]
    return pl.pallas_call(
        functools.partial(leaf_kernel, per_step, slots, blocks),
        out_shape=(
            jax.ShapeDtypeStruct((cells, rows, width), BF16),
            jax.ShapeDtypeStruct((blocks, rows, sw), F32),
        )
        + (jax.ShapeDtypeStruct((blocks, rows, sw), BF16),) * 2
        + tuple(jax.ShapeDtypeStruct((n, rows, sw), BF16) for n in parts),
        grid_spec=pltpu.PrefetchScalarGridSpec(
            num_scalar_prefetch=1,
            grid=(cells // per_step,),
            in_specs=[
                pl.BlockSpec((per_step, rows, width), by_cell),
                pl.BlockSpec((per_step, width, width), by_cell),
                pl.BlockSpec((per_step, slots, width, sw), lambda i, *_: (i, 0, 0, 0)),
            ],
            out_specs=[pl.BlockSpec((per_step, rows, width), by_cell)] + [summed] * 3
            + [pl.BlockSpec((n, rows, sw), whole, pipeline_mode=pl.Buffered(1)) for n in parts],
            scratch_shapes=[pltpu.VMEM((spans * blocks, rows, sw), F32)],
        ),
        compiler_params=pltpu.CompilerParams(vmem_limit_bytes=60 << 20),
        cost_estimate=pl.CostEstimate(flops=0, bytes_accessed=0, transcendentals=0),
        name="leaf",
    )(targets, right_side, leaf_inverse, leaf_couple)


def add_kernel(near_ref, *refs):
    *part_refs, out_ref = refs
    at = 0
    for ref in part_refs:
        count = ref.shape[0]
        mine = near_ref[pl.ds(at, count)].astype(F32)
        out_ref[pl.ds(at, count)] = (mine + ref[...].astype(F32)).astype(BF16)
        at += count


def add_parts(near, *parts):
    vmem = pl.BlockSpec(memory_space=pltpu.VMEM)
    return pl.pallas_call(
        add_kernel,
        out_shape=jax.ShapeDtypeStruct(near.shape, BF16),
        in_specs=[vmem] * (1 + len(parts)),
        out_specs=vmem,
        compiler_params=pltpu.CompilerParams(vmem_limit_bytes=16 << 20),
        cost_estimate=pl.CostEstimate(flops=0, bytes_accessed=0, transcendentals=0),
        name="add_parts",
    )(near, *parts)


def lift_kernel(base_ref, far_ref, near_ref, own_ref, prev_ref, next_ref, opp_lo_ref, opp_hi_ref, out_ref):
    blocks, rows, width = base_ref.shape
    sw = own_ref.shape[1]
    deep = opp_lo_ref.shape[0]
    depth = 2 * width
    column = lax.axis_index("rhs")
    total = jnp.zeros((rows, 4 * sw), F32)
    for b in range(0, blocks, 2):
        parts = [
            (base_ref[k] - far_ref[k].astype(F32) - near_ref[k].astype(F32)).astype(BF16) for k in (b, b + 1)
        ]
        row = b * width
        pieces = [ref[row : row + depth, :] for ref in (own_ref, prev_ref, next_ref)]
        opp_ref = (opp_lo_ref, opp_hi_ref)[row // deep]
        pieces.append(opp_ref[row % deep : row % deep + depth, :])
        total = total + dot32(jnp.concatenate(parts, axis=1), jnp.concatenate(pieces, axis=1))
    result = total.astype(BF16)
    for j, turn in enumerate((0, 3, 1, 2)):
        at = pl.multiple_of((column + turn) % 4 * sw, sw)
        out_ref[:, pl.ds(at, sw)] = result[:, j * sw : (j + 1) * sw]


def lift_phase(*operands):
    rows, cols = operands[0].shape[1], operands[3].shape[1]
    vmem = pl.BlockSpec(memory_space=pltpu.VMEM)
    return pl.pallas_call(
        lift_kernel,
        out_shape=jax.ShapeDtypeStruct((rows, 4 * cols), BF16),
        in_specs=[vmem] * len(operands),
        out_specs=vmem,
        compiler_params=pltpu.CompilerParams(vmem_limit_bytes=24 << 20),
        cost_estimate=pl.CostEstimate(flops=0, bytes_accessed=0, transcendentals=0),
        name="lift",
    )(*operands)


def assemble_kernel(with_product, own_ref, prev_ref, next_ref, opp_ref, ops_ref, *rest):
    sw = own_ref.shape[1]
    column = lax.axis_index("rhs")
    for turn, ref in ((0, own_ref), (3, prev_ref), (1, next_ref), (2, opp_ref)):
        ops_ref[:, pl.ds(pl.multiple_of((column + turn) % 4 * sw, sw), sw)] = ref[...]
    if with_product:
        (product_ref,) = rest
        width = ops_ref.shape[1]
        for r in range(0, 2 * width, width // 2):
            rows = pl.ds(r, width // 2)
            product_ref[rows, :] = (-dot32(ops_ref[rows, :], ops_ref[pl.ds(2 * width, width), :])).astype(BF16)


def assemble(pieces, with_product):
    depth, cols = pieces[0].shape
    outs = [jax.ShapeDtypeStruct((depth, 4 * cols), BF16)]
    if with_product:
        outs.append(jax.ShapeDtypeStruct((8 * cols, 4 * cols), BF16))
    vmem = pl.BlockSpec(memory_space=pltpu.VMEM)
    return pl.pallas_call(
        functools.partial(assemble_kernel, with_product),
        out_shape=tuple(outs),
        in_specs=[vmem] * 4,
        out_specs=tuple([vmem] * len(outs)),
        compiler_params=pltpu.CompilerParams(vmem_limit_bytes=16 << 20),
        cost_estimate=pl.CostEstimate(
            flops=0, bytes_accessed=0, transcendentals=0
        ),
        name="assemble_product" if with_product else "assemble",
    )(*pieces)


def top_kernel(first_ref, second_ref, ops_q_ref, ops_p_ref, sol_ref, skel_ref):
    width = first_ref.shape[1]

    def merge(first, second, ops_ref):
        sol = (dot32(first, ops_ref[pl.ds(0, width), :]) + dot32(second, ops_ref[pl.ds(width, width), :])).astype(BF16)
        skel = 0.5 * (first.astype(F32) + second.astype(F32)) - dot32(sol, ops_ref[pl.ds(2 * width, width), :])
        return sol, skel

    level_sol, level_skel = merge(first_ref[...], second_ref[...], ops_q_ref)
    sol, skel = merge(level_skel.astype(BF16), level_sol, ops_p_ref)
    sol_ref[...] = sol
    skel_ref[...] = skel


def top_phase(first, second, ops_q, ops_p):
    rows, width = first.shape
    vmem = pl.BlockSpec(memory_space=pltpu.VMEM)
    return pl.pallas_call(
        top_kernel,
        out_shape=(jax.ShapeDtypeStruct((rows, width), BF16), jax.ShapeDtypeStruct((rows, width), F32)),
        in_specs=[vmem] * 4,
        out_specs=(vmem, vmem),
        compiler_params=pltpu.CompilerParams(vmem_limit_bytes=16 << 20),
        cost_estimate=pl.CostEstimate(flops=400_000_000, bytes_accessed=4_000_000, transcendentals=0),
        name="top",
    )(first, second, ops_q, ops_p)


def on_device(
    right_side, leaf_inverse, leaf_couple, skel_target, skeleton_in, lift_ops, node_mix, node_couple
):
    count = lax.axis_size("cells")
    levels = count.bit_length() - 1
    rows, blocks, width = skeleton_in.shape

    lift = lift_ops[0]
    deep = lift.shape[0] // 2
    prev = shifted(lift, "rhs", 1)
    following = shifted(lift, "rhs", -1)

    solved, own, far, near, *parts = leaf_phase(skel_target, right_side, leaf_inverse, leaf_couple, blocks)

    half = range(count // 2)
    swap = [(2 * c, 2 * c + 1) for c in half] + [(2 * c + 1, 2 * c) for c in half]
    dest, red = parts[: len(DEST_PARTS)], parts[len(DEST_PARTS) :]
    red_in = [along_pairs(part, swap) for part in red]
    far_in = along_pairs(far, [(2 * c + 1, 2 * c + 3) for c in half] + [(2 * c, 2 * c - 2) for c in half])
    near = add_parts(near, *red_in)
    near_in = along_pairs(near, [(2 * c + 1, 2 * c + 2) for c in half] + [(2 * c, 2 * c - 1) for c in half])

    *dest, prev, following = lax.optimization_barrier((*dest, prev, following))
    opp_lo = shifted(prev[:deep], "rhs", 1)
    opp_hi = shifted(following[deep:], "rhs", -1)
    dest_in = jnp.concatenate([along_pairs(part, swap) for part in dest], axis=0)
    dest_in, far_in, near_in = lax.optimization_barrier((dest_in, far_in, near_in))
    base = lax.optimization_barrier(jnp.transpose(skeleton_in, (1, 0, 2)) - own - dest_in.astype(F32))
    current = lift_phase(base, far_in, near_in, lift, prev, following, opp_lo, opp_hi)
    base_after, far_after, near_after, _ = lax.optimization_barrier((base, far_in, near_in, current))
    skeleton_rhs = jnp.transpose(base_after - far_after.astype(F32) - near_after.astype(F32), (1, 0, 2))

    mix, couple, _ = lax.optimization_barrier((node_mix, node_couple, near))
    node_ops = jnp.concatenate([mix[0], couple[0]], axis=0)
    node_ops, _ = lax.optimization_barrier((node_ops, base))
    ops_prev = shifted(node_ops, "rhs", 1)
    ops_next = shifted(node_ops, "rhs", -1)
    far_ops, _ = lax.optimization_barrier((node_ops, current))
    across = shifted(far_ops, "cells", count // 2)
    ops_opp = shifted(node_ops, "rhs", 2)
    ops_p, product = assemble((node_ops, ops_prev, ops_next, ops_opp), True)

    mw = current.shape[1]
    for level in range(1, levels):
        distance = max(1, 2 ** (level - 2))
        first = shifted(current, "cells", distance)
        second = current if level == 1 else shifted(current, "cells", -distance)
        if level == 1:
            first, product, across = lax.optimization_barrier((first, product, across))
        if level == levels - 1:
            first, ops_q = lax.optimization_barrier((first, ops_q))
        skel = 0.5 * (first.astype(F32) + second.astype(F32)) + (
            dot32(first, product[:mw]) + dot32(second, product[mw:])
        )
        current = skel.astype(BF16)
        if level == 2:
            across, _ = lax.optimization_barrier((across, current))
            ops_q = assemble((across, *(shifted(across, "rhs", turn) for turn in (1, -1, 2))), False)[0]
    distance = 2 ** (levels - 2)
    second = shifted(current, "cells", distance)
    first = shifted(current, "cells", -distance)
    node_solution, node_skeleton = top_phase(first, second, ops_q, ops_p)
    return (solved, skeleton_rhs, node_solution[None], node_skeleton[None])


def solution(mesh):
    return jax.shard_map(
        on_device,
        mesh=mesh,
        in_specs=(
            P("cells", "rhs", None),
            P("cells", None, None),
            P("cells", None, None, None),
            P("cells", None),
            P("rhs", "cells", None),
            P("cells", None, "rhs"),
            P("cells", None, "rhs"),
            P("cells", None, "rhs"),
        ),
        out_specs=(
            P("cells", "rhs", None),
            P("rhs", "cells", None),
            P("cells", "rhs", None),
            P("cells", "rhs", None),
        ),
        check_vma=False,
    )
```
